32 devices in a mesh: gx: 4 (over z), gy: 4 (over x, core), gz: 2 (over y).
Axes of the slice: x: 2, y: 2, z: 4, core: 2. Of those that a mesh axis runs over, the one named last changes fastest.
Arguments:
- features: float32 [4, 8, 2, 128, 256], P('gx', 'gy', 'gz'), may hold values from -82 to 82
- occupancy: int32 [4, 8, 2], P('gx', 'gy', 'gz'), may hold values from 1 to 128, as said below
- dest_bin: int32 [4, 8, 2], P('gx', 'gy', 'gz'), may hold values from 0 to 63, as said below
- query_weight: bfloat16 [256, 256], replicated, may hold values from -0.375 to 0.375
- key_weight: bfloat16 [256, 256], replicated, may hold values from -0.375 to 0.375
- value_weight: bfloat16 [256, 256], replicated, may hold values from -0.375 to 0.375
- out_weight: bfloat16 [256, 256], replicated, may hold values from -0.375 to 0.375
- up_weight: bfloat16 [256, 1024], replicated, may hold values from -0.375 to 0.375
- down_weight: bfloat16 [1024, 256], replicated, may hold values from -0.1875 to 0.1875
- attention_gain: float32 [256], replicated, may hold values from 0.25 to 1.75
- feed_gain: float32 [256], replicated, may hold values from 0.25 to 1.75
Outputs:
- particles: float32 [4, 8, 2, 128, 256], P('gx', 'gy', 'gz')
The draws below stay inside these ranges and needn't reach their ends.
Inputs may be any that keep to these rules, and one draw needn't show every extreme that they name: `occupancy`: some bin holds 128 live particles. `dest_bin`: A permutation of the bins; every block stays on a device with the same gx and gy index, and each device sends at most 1 block to any one device, a bound that some pair of devices reaches.
All inputs are finite; a program needn't handle non-finite values.
Results may differ from the reference program's by a relative error of at most 0.0065.
The reference program's roundings to bfloat16 on the way (of `rows`, `query`, `weights`, `attended` and `inner`) count: a program that leaves them out, or rounds other values in their place, can miss the bound.
Values may be sent and summed in bfloat16 or wider, within the bound.
No kernel may reach another device: no remote copies, remote signals or barrier semaphores. Data moves between devices by JAX's collectives and lax.ppermute only.
A program may use at most 64 MiB of HBM per device.

```python
import jax
import jax.numpy as jnp
from jax import lax

W = 256
HEADS = 8
FF = 1024
P_SIZE = 128
BX = 1
BY = 2
BZ = 1
LAYERS = 2
NBX = 4
NBY = 8
NBZ = 2


def draw_features(key, part):
    shape = (NBX, NBY, NBZ, P_SIZE, W)
    key_base = jax.random.fold_in(key, 0)
    return jnp.clip(jax.random.normal(key_base, shape, jnp.float32), -6.0, 6.0)


def draw_occupancy(key, part):
    drawn = jax.random.randint(key, (NBX, NBY, NBZ), 1, P_SIZE + 1)
    return drawn.at[0, 0, 0].set(P_SIZE).astype(jnp.int32)


def line_permutation(key, length):
    return jax.random.permutation(key, length)


def draw_dest_bin(key, part):
    lines_x = NBX // BX
    lines_y = NBY // BY
    depth = NBZ // BZ
    count = BX * BY * BZ
    lines = lines_x * lines_y
    key_shift, key_place = jax.random.split(key)
    shifts = jax.vmap(lambda k: line_permutation(k, depth))(jax.random.split(key_shift, lines))
    order = jnp.arange(count, dtype=jnp.int32) % depth
    shift = shifts[:, order]
    place = jax.vmap(lambda k: line_permutation(k, count))(jax.random.split(key_place, lines * depth)).reshape(lines, depth, count)
    source_z = jnp.arange(depth, dtype=jnp.int32)[None, :, None]
    target_z = (source_z + shift[:, None, :]) % depth
    target_local = jnp.take_along_axis(place, target_z, axis=1)
    local_x = target_local // (BY * BZ)
    local_y = target_local // BZ % BY
    local_z = target_local % BZ
    line_x = (jnp.arange(lines, dtype=jnp.int32) // lines_y)[:, None, None]
    line_y = (jnp.arange(lines, dtype=jnp.int32) % lines_y)[:, None, None]
    flat = ((line_x * BX + local_x) * NBY + line_y * BY + local_y) * NBZ + target_z * BZ + local_z
    grid = flat.reshape(lines_x, lines_y, depth, BX, BY, BZ).transpose(0, 3, 1, 4, 2, 5).reshape(NBX, NBY, NBZ)
    return grid.astype(jnp.int32)


def noise(stream_key, shape, scale, reach, kind=jnp.bfloat16):
    return jnp.clip(scale * jax.random.normal(stream_key, shape, jnp.float32), -reach, reach).astype(kind)


def setup_inputs(seed: int = 0) -> dict:
    seeds = jax.random.split(jax.random.key(seed), 12)
    return {
        "features": draw_features(jax.random.fold_in(seeds[11], 71), 0),
        "occupancy": draw_occupancy(jax.random.fold_in(seeds[11], 71), 0),
        "dest_bin": draw_dest_bin(jax.random.fold_in(seeds[11], 71), 0),
        "query_weight": noise(seeds[3], (W, W), W ** -0.5, 0.375),
        "key_weight": noise(seeds[4], (W, W), W ** -0.5, 0.375),
        "value_weight": noise(seeds[5], (W, W), W ** -0.5, 0.375),
        "out_weight": noise(seeds[6], (W, W), W ** -0.5, 0.375),
        "up_weight": noise(seeds[7], (W, FF), W ** -0.5, 0.375),
        "down_weight": noise(seeds[8], (FF, W), FF ** -0.5, 0.1875),
        "attention_gain": jnp.clip(1.0 + 0.15 * jax.random.normal(seeds[9], (W,), jnp.float32), 0.25, 1.75),
        "feed_gain": jnp.clip(1.0 + 0.15 * jax.random.normal(seeds[10], (W,), jnp.float32), 0.25, 1.75),
    }


EPSILON = 1e-05

def layer_norm(values, gain):
    centre = values - lax.optimization_barrier(jnp.mean(values, axis=-1, keepdims=True))
    spread = lax.optimization_barrier(jnp.mean(centre * centre, axis=-1, keepdims=True))
    return centre * lax.rsqrt(spread + EPSILON) * gain

def neighbours(padded):
    parts = [padded[1:-1, 1:-1, 1:-1], padded[:-2, 1:-1, 1:-1], padded[2:, 1:-1, 1:-1], padded[1:-1, :-2, 1:-1], padded[1:-1, 2:, 1:-1], padded[1:-1, 1:-1, :-2], padded[1:-1, 1:-1, 2:]]
    return jnp.stack(parts, axis=3)

def attend(query, keys, values, mask, heads):
    batch, slots, width = query.shape
    head_size = width // heads
    total_keys = keys.shape[1]
    query_heads = query.astype(jnp.float32).reshape(batch, slots, heads, head_size)
    key_heads = keys.astype(jnp.float32).reshape(batch, total_keys, heads, head_size)
    value_heads = values.astype(jnp.float32).reshape(batch, total_keys, heads, head_size)
    scores = jnp.einsum('bqhd,bkhd->bhqk', query_heads, key_heads) * head_size ** (-0.5)
    valid = mask[:, None, None, :]
    scores = jnp.where(valid, scores, -1e+30)
    peak = lax.optimization_barrier(jnp.max(scores, axis=-1, keepdims=True))
    weights = jnp.where(valid, jnp.exp(scores - peak), 0.0)
    weights = (weights / lax.optimization_barrier(jnp.sum(weights, axis=-1, keepdims=True))).astype(jnp.bfloat16)
    mixed = jnp.einsum('bhqk,bkhd->bqhd', weights.astype(jnp.float32), value_heads)
    return mixed.astype(jnp.bfloat16).reshape(batch, slots, width)

def update(rows, attended, occupied, out_weight, up_weight, down_weight, attention_gain, feed_gain):
    batch, slots, width = rows.shape
    mixed = jnp.dot(attended.reshape(-1, width), out_weight, preferred_element_type=jnp.float32)
    hidden = layer_norm(rows.reshape(-1, width) + mixed, attention_gain)
    inner = jax.nn.gelu(jnp.dot(hidden.astype(jnp.bfloat16), up_weight, preferred_element_type=jnp.float32)).astype(jnp.bfloat16)
    grown = jnp.dot(inner, down_weight, preferred_element_type=jnp.float32)
    result = layer_norm(hidden + grown, feed_gain).reshape(batch, slots, width)
    live = jnp.arange(slots, dtype=jnp.int32)[None, :, None] < occupied[:, None, None]
    return jnp.where(live, result, 0.0)

def apply_layer(state, counts, query_weight, key_weight, value_weight, out_weight, up_weight, down_weight, attention_gain, feed_gain):
    grid_x, grid_y, grid_z, slots, width = state.shape
    flat = state.astype(jnp.bfloat16).reshape(-1, width)
    query = jnp.dot(flat, query_weight, preferred_element_type=jnp.float32).astype(jnp.bfloat16).reshape(state.shape)
    keyval = jnp.concatenate([jnp.dot(flat, key_weight, preferred_element_type=jnp.float32), jnp.dot(flat, value_weight, preferred_element_type=jnp.float32)], axis=1)
    keyval = keyval.astype(jnp.bfloat16).reshape(grid_x, grid_y, grid_z, slots, 2 * width)
    padded = jnp.pad(keyval, ((1, 1), (1, 1), (1, 1), (0, 0), (0, 0)))
    padded_counts = jnp.pad(counts, 1)

    def column(index):
        pos_x = (index // grid_y).astype(jnp.int32)
        pos_y = (index % grid_y).astype(jnp.int32)
        zero = jnp.zeros((), jnp.int32)
        block = lax.dynamic_slice(padded, (pos_x, pos_y, zero, zero, zero), (3, 3, grid_z + 2, slots, 2 * width))
        block_counts = lax.dynamic_slice(padded_counts, (pos_x, pos_y, zero), (3, 3, grid_z + 2))
        keys_here = neighbours(block)[0, 0].reshape(grid_z, 7 * slots, 2 * width)
        near = neighbours(block_counts)[0, 0]
        mask = (jnp.arange(slots, dtype=jnp.int32)[None, None, :] < near[:, :, None]).reshape(grid_z, 7 * slots)
        query_here = lax.dynamic_slice(query, (pos_x, pos_y, zero, zero, zero), (1, 1, grid_z, slots, width))[0, 0]
        rows_here = lax.dynamic_slice(state, (pos_x, pos_y, zero, zero, zero), (1, 1, grid_z, slots, width))[0, 0]
        count_here = lax.dynamic_slice(counts, (pos_x, pos_y, zero), (1, 1, grid_z))[0, 0]
        attended = attend(query_here, keys_here[..., :width], keys_here[..., width:], mask, HEADS)
        return update(rows_here, attended, count_here, out_weight, up_weight, down_weight, attention_gain, feed_gain)
    result = lax.map(column, jnp.arange(grid_x * grid_y, dtype=jnp.int32))
    return result.reshape(state.shape)

def migrate(state, counts, dest_bin):
    slots, width = (state.shape[3], state.shape[4])
    targets = dest_bin.reshape(-1).astype(jnp.int32)
    moved = jnp.zeros((targets.shape[0], slots, width), state.dtype).at[targets].set(state.reshape(-1, slots, width))
    moved_counts = jnp.zeros(targets.shape, counts.dtype).at[targets].set(counts.reshape(-1))
    return (moved.reshape(state.shape), moved_counts.reshape(counts.shape))

def reference(features, occupancy, dest_bin, query_weight, key_weight, value_weight, out_weight, up_weight, down_weight, attention_gain, feed_gain):
    state, counts = (features, occupancy)
    for layer in range(LAYERS):
        state = apply_layer(state, counts, query_weight, key_weight, value_weight, out_weight, up_weight, down_weight, attention_gain, feed_gain)
        if layer + 1 < LAYERS:
            state, counts = migrate(state, counts, dest_bin)
    return state
```

```python
import functools

import jax
import jax.numpy as jnp
from jax import lax
from jax.experimental import pallas as pl
from jax.experimental.pallas import tpu as pltpu
from jax.sharding import PartitionSpec as P

HEADS = 8
LAYERS = 2
EPSILON = 1e-05
LOG2E = 1.4426950408889634
DEAD = -1e30
HEAD_ROWS = 16

F32 = jnp.float32
BF16 = jnp.bfloat16

VMEM = pl.BlockSpec(memory_space=pltpu.VMEM)
SMEM = pl.BlockSpec(memory_space=pltpu.SMEM)


def call(body, outs, specs, name, limit=24 << 20):
    return pl.pallas_call(
        body,
        out_shape=outs,
        in_specs=specs,
        out_specs=jax.tree.map(lambda _: VMEM, outs),
        compiler_params=pltpu.CompilerParams(vmem_limit_bytes=limit),
        name=name,
    )


def swaps(count, parity):
    pairs = []
    for low in range(parity, count - 1, 2):
        pairs += [(low, low + 1), (low + 1, low)]
    return pairs


def dot(a, b):
    return jnp.dot(a, b, preferred_element_type=F32)


def layer_norm(values, gain):
    centre = values - jnp.mean(values, axis=-1, keepdims=True)
    spread = jnp.mean(centre * centre, axis=-1, keepdims=True)
    return centre * lax.rsqrt(spread + EPSILON) * gain


def header(count, role, width):
    row = lax.broadcasted_iota(jnp.int32, (HEAD_ROWS, width), 0)
    return jnp.where(row == 1, role, count).astype(F32).astype(BF16)


def live_rows(block, slots):
    count = block[slots : slots + 1, :128].astype(F32)
    row = lax.broadcasted_iota(jnp.int32, (slots, 128), 0).astype(F32)
    return row < count


def pack_body(features, counts, both, first, second):
    slots, width = features.shape[1:]
    parity = lax.axis_index("gy") % 2
    for role, single in ((0, first), (1, second)):
        held = 1 - parity if role == 0 else parity
        rows = features[held].astype(BF16)
        top = header(counts[held], role, width)
        both[role, :slots] = rows
        both[role, slots:] = top
        single[:slots] = rows
        single[slots:] = top


def pack(features, counts):
    bins, slots, width = features.shape
    tall = slots + HEAD_ROWS
    outs = [
        jax.ShapeDtypeStruct((bins, tall, width), BF16),
        jax.ShapeDtypeStruct((tall, width), BF16),
        jax.ShapeDtypeStruct((tall, width), BF16),
    ]
    return call(pack_body, outs, [VMEM, SMEM], "pack")(features, counts)


def layer_body(kind, spans, refs, outs):
    (residual, own, halos, sides, weights, gains, extra) = refs
    (query_weight, key_weight, value_weight, out_weight, up_weight, down_weight) = weights
    slots, width = residual.shape[1:]
    head_size = width // HEADS
    groups = width // 128
    per_group = HEADS // groups
    parity = lax.axis_index("gy") % 2
    factor = head_size ** (-0.5) * LOG2E

    flat_rows = []
    lives = []
    for block in (own[0], own[1]):
        flat_rows.append(block[:slots])
        lives.append(live_rows(block, slots))
    for role in range(2):
        for halo in halos:
            block = halo[role]
            flat_rows.append(block[:slots])
            lives.append(live_rows(block, slots))
        block = sides[role][...]
        flat_rows.append(block[:slots])
        lives.append(live_rows(block, slots))
    every = jnp.concatenate(flat_rows, axis=0)
    keys = dot(every, key_weight[...]).astype(BF16)
    values = dot(every, value_weight[...]).astype(BF16)
    queries = dot(jnp.concatenate(flat_rows[:2], axis=0), query_weight[...]).astype(BF16)
    near = len(halos) + 1
    lane = lax.broadcasted_iota(jnp.int32, (slots, 128), 1)
    mark = jnp.where(lane == 0, 1.0, 0.0).astype(BF16)

    attended = []
    for role in range(2):
        picks = [0, 1] + [2 + role * near + n for n in range(near)]

        def gather(array, column, span):
            return jnp.concatenate(
                [array[p * slots : (p + 1) * slots, column : column + span] for p in picks], axis=0
            )

        bias = jnp.concatenate(
            [jnp.where(lives[p], 0.0, DEAD).astype(BF16) for p in picks], axis=0
        )
        mine = gather(values, 0, width)
        query = queries[role * slots : (role + 1) * slots]
        total = None
        for group in range(groups):
            key = jnp.concatenate([gather(keys, group * 128, 128), bias], axis=1)
            for inner in range(per_group):
                head = group * per_group + inner
                inside = (lane >= inner * head_size) & (lane < (inner + 1) * head_size)
                part = query[:, group * 128 : (group + 1) * 128]
                part = jnp.where(inside, part.astype(F32), 0.0).astype(BF16)
                scores = lax.dot_general(
                    jnp.concatenate([part, mark], axis=1),
                    key,
                    (((1,), (1,)), ((), ())),
                    preferred_element_type=F32,
                )
                peak = jnp.max(scores, axis=-1, keepdims=True)
                power = jnp.exp2((scores - peak) * factor)
                scale = 1.0 / jnp.sum(power, axis=-1, keepdims=True)
                mixed = dot((power * scale).astype(BF16), mine)
                column = lax.broadcasted_iota(jnp.int32, (slots, width), 1)
                inside = (column >= head * head_size) & (column < (head + 1) * head_size)
                mixed = jnp.where(inside, mixed, 0.0)
                total = mixed if total is None else total + mixed
        attended.append(total.astype(BF16))
    attended = jnp.concatenate(attended, axis=0)

    attention_gain, feed_gain = gains
    if kind == "features":
        rows = jnp.concatenate([residual[1 - parity], residual[parity]], axis=0)
    else:
        rows = jnp.concatenate([residual[0], residual[1]], axis=0)
    hidden = layer_norm(rows + dot(attended, out_weight[...]), attention_gain[...])
    inner = jax.nn.gelu(dot(hidden.astype(BF16), up_weight[...])).astype(BF16)
    result = layer_norm(hidden + dot(inner, down_weight[...]), feed_gain[...])
    row = lax.broadcasted_iota(jnp.int32, (slots, width), 0).astype(F32)
    results = []
    for role in range(2):
        count = own[role, slots : slots + 1, :].astype(F32)
        results.append(
            jnp.where(row < count, result[role * slots : (role + 1) * slots], 0.0)
        )

    if outs[0] == "bins":
        (out,) = outs[1:]
        out[1 - parity] = results[0]
        out[parity] = results[1]
        return
    travel, stayed = outs[1:]
    places = extra
    span_y, span_z = spans
    for role in range(2):
        held = 1 - parity if role == 0 else parity
        place = places[held]
        stays = place % span_z == lax.axis_index("gz")
        target = (place // span_z) % 2
        new_role = jnp.where(target == parity, 1, 0)
        slot = jnp.where(stays, 1, 0)
        travel[slot, :slots] = results[role].astype(BF16)
        top = own[role, slots:].astype(F32)
        line = lax.broadcasted_iota(jnp.int32, (HEAD_ROWS, width), 0)
        travel[slot, slots:] = jnp.where(line == 1, new_role.astype(F32), top).astype(BF16)

        @pl.when(stays)
        def _():
            stayed[...] = results[role]


def run_layer(kind, end, spans, residual, own, halos, sides, weights, gains, places=None):
    bins, slots, width = residual.shape
    tall = slots + HEAD_ROWS
    n_halo = len(halos)
    if end == "bins":
        outs = [jax.ShapeDtypeStruct((bins, slots, width), F32)]
    else:
        outs = [
            jax.ShapeDtypeStruct((bins, tall, width), BF16),
            jax.ShapeDtypeStruct((slots, width), F32),
        ]
    args = [residual, own, *halos, *sides, *weights, *gains]
    specs = [VMEM] * len(args)
    if end != "bins":
        args.append(places)
        specs.append(SMEM)

    def body(*refs):
        ins, results = refs[: len(args)], refs[len(args) :]
        at = 2 + n_halo
        layer_body(
            kind,
            spans,
            (
                ins[0],
                ins[1],
                ins[2:at],
                ins[at : at + 2],
                ins[at + 2 : at + 8],
                ins[at + 8 : at + 10],
                ins[at + 10] if end != "bins" else None,
            ),
            (end, *results),
        )

    return call(body, outs, specs, f"layer_{kind}_{end}")(*args)


def choose(role, yes, no):
    return jnp.where(role < 0.5, yes.astype(F32), no.astype(F32))


def settle_body(travel, arrived, stayed, both, first, second, beside, residual):
    slots, width = stayed.shape
    stay, came = travel[1], arrived[0]
    role = stay[slots + 1 : slots + 2].astype(F32)
    for index, single in ((0, first), (1, second)):
        block = choose(role, *((stay, came) if index == 0 else (came, stay))).astype(BF16)
        both[index] = block
        single[...] = block
        rows = stayed[...], came[:slots]
        residual[index] = choose(role, *(rows if index == 0 else rows[::-1]))
    peer, left = arrived[1], travel[0]
    role = peer[slots + 1 : slots + 2].astype(F32)
    beside[0] = choose(role, peer, left).astype(BF16)
    beside[1] = choose(role, left, peer).astype(BF16)


def settle(travel, arrived, stayed):
    bins, tall, width = travel.shape
    slots = stayed.shape[0]
    outs = [
        jax.ShapeDtypeStruct((bins, tall, width), BF16),
        jax.ShapeDtypeStruct((tall, width), BF16),
        jax.ShapeDtypeStruct((tall, width), BF16),
        jax.ShapeDtypeStruct((bins, tall, width), BF16),
        jax.ShapeDtypeStruct((bins, slots, width), F32),
    ]
    return call(settle_body, outs, [VMEM] * 3, "settle")(travel, arrived, stayed)


def relocate(state, counts, dest_bin, bins_y):
    total, slots, width = state.shape
    depth = lax.axis_size("gz")
    targets = dest_bin.reshape(-1)
    peer = targets % depth
    local = targets // depth % bins_y
    order = jnp.arange(total, dtype=jnp.int32)
    earlier = (peer[None, :] == peer[:, None]) & (order[None, :] < order[:, None])
    slot = jnp.sum(earlier.astype(jnp.int32), axis=1)
    capacity = (total + depth - 1) // depth
    outgoing = jnp.zeros((depth, capacity, slots, width), F32).at[peer, slot].set(state)
    outgoing_counts = jnp.zeros((depth, capacity), jnp.int32).at[peer, slot].set(counts)
    outgoing_places = jnp.full((depth, capacity), total, jnp.int32).at[peer, slot].set(local)
    arrived = lax.all_to_all(outgoing.astype(BF16), "gz", 0, 0, tiled=True).astype(F32)
    arrived_counts = lax.all_to_all(outgoing_counts, "gz", 0, 0, tiled=True)
    places = lax.all_to_all(outgoing_places, "gz", 0, 0, tiled=True).reshape(-1)
    moved = jnp.zeros((total, slots, width), F32)
    moved = moved.at[places].set(arrived.reshape(-1, slots, width), mode="drop")
    moved_counts = jnp.zeros((total,), jnp.int32)
    moved_counts = moved_counts.at[places].set(arrived_counts.reshape(-1), mode="drop")
    return moved, moved_counts


def line_halo(block, axis):
    count = lax.axis_size(axis)
    return [lax.ppermute(block, axis, swaps(count, p)) for p in range(2) if swaps(count, p)]


def shards(features, occupancy, dest_bin, *rest):
    weights, gains = rest[:6], tuple(g.reshape(1, -1) for g in rest[6:])
    shape = features.shape
    slots, width = shape[3:]
    state = features.reshape(2, slots, width)
    counts = occupancy.reshape(2)
    places = dest_bin.reshape(2)
    depth = lax.axis_size("gz")
    spans = (2 * lax.axis_size("gy"), depth)
    side = lax.axis_size("gy")

    def sideways(first, second):
        return [
            lax.ppermute(block, "gy", swaps(side, p)) for p, block in ((0, first), (1, second))
        ]

    own, first, second = pack(state, counts)
    halos = line_halo(own, "gx") + line_halo(own, "gz")
    sides = sideways(first, second)
    if depth == 2:
        travel, stayed = run_layer(
            "features", "travel", spans, state, own, halos, sides, weights, gains, places
        )
        arrived = lax.ppermute(travel, "gz", swaps(depth, 0))
        own, first, second, beside, residual = settle(travel, arrived, stayed)
        halos = line_halo(own, "gx") + [beside]
        sides = sideways(first, second)
        (out,) = run_layer(
            "settled", "bins", spans, residual, own, halos, sides, weights, gains
        )
    else:
        (state,) = run_layer(
            "features", "bins", spans, state, own, halos, sides, weights, gains
        )
        state, counts = relocate(state, counts, places, 2)
        own, first, second = pack(state, counts)
        halos = line_halo(own, "gx") + line_halo(own, "gz")
        sides = sideways(first, second)
        (out,) = run_layer(
            "features", "bins", spans, state, own, halos, sides, weights, gains
        )
    return out.reshape(shape)


def solution(mesh):
    placed = (
        P("gx", "gy", "gz", None, None),
        P("gx", "gy", "gz"),
        P("gx", "gy", "gz"),
        *([P()] * 8),
    )
    return jax.shard_map(
        shards,
        mesh=mesh,
        in_specs=placed,
        out_specs=P("gx", "gy", "gz", None, None),
        check_vma=False,
    )
```

```python
import jax
import jax.numpy as jnp
from jax import lax
from jax.experimental import pallas as pl
from jax.experimental.pallas import tpu as pltpu
from jax.sharding import PartitionSpec as P

HEADS = 8
EPSILON = 1e-05
LOG2E = 1.4426950408889634
DEAD = -1e30
HEAD_ROWS = 16
ROLES = 2

F32 = jnp.float32
BF16 = jnp.bfloat16

VMEM = pl.BlockSpec(memory_space=pltpu.VMEM)
SMEM = pl.BlockSpec(memory_space=pltpu.SMEM)
ROWS = (((1,), (1,)), ((), ()))
COLUMNS = (((0,), (1,)), ((), ()))
TURNED = (((0,), (0,)), ((), ()))


def shape(dims, dtype):
    return jax.ShapeDtypeStruct(dims, dtype)


def call(body, outs, specs, scratch=(), limit=30 << 20):
    return pl.pallas_call(
        body,
        out_shape=outs,
        in_specs=specs,
        out_specs=jax.tree.map(lambda _: VMEM, outs),
        scratch_shapes=scratch,
        compiler_params=pltpu.CompilerParams(vmem_limit_bytes=limit),
    )


def swaps(count, parity, around=False):
    pairs = []
    for low in range(parity, count - 1, 2):
        pairs += [(low, low + 1), (low + 1, low)]
    if around and parity == 1 and count % 2 == 0 and count > 2:
        pairs += [(0, count - 1), (count - 1, 0)]
    return pairs


def dot(a, b, dims=(((1,), (0,)), ((), ()))):
    return lax.dot_general(a, b, dims, preferred_element_type=F32)


def layer_norm(values, gain):
    centre = values - jnp.mean(values, axis=-1, keepdims=True)
    spread = jnp.mean(centre * centre, axis=-1, keepdims=True)
    return centre * lax.rsqrt(spread + EPSILON) * gain


def live_rows(block, slots, present=None):
    count = block[slots : slots + 1, :128].astype(F32)
    if present is not None:
        count = jnp.where(present, count, 0.0)
    row = lax.broadcasted_iota(jnp.int32, (slots, 128), 0).astype(F32)
    return jnp.where(row < count, 0.0, DEAD).astype(BF16)


def prepare_body(out):
    out[...] = jnp.zeros_like(out)


def prepare(slots, width):
    return pl.pallas_call(
        prepare_body,
        out_shape=shape((8, 128), F32),
        out_specs=VMEM,
        compiler_params=pltpu.CompilerParams(vmem_limit_bytes=1 << 20),
        cost_estimate=pl.CostEstimate(
            flops=80000 * slots * width, transcendentals=0, bytes_accessed=0
        ),
        name="prepare",
    )()


def pack_body(features, counts, ready, both, first, second, residual):
    slots, width = features.shape[1:]
    parity = lax.axis_index("gy") % 2
    del ready
    for role, single in ((0, first), (1, second)):
        held = 1 - parity if role == 0 else parity
        state = features[held]
        residual[role] = state
        rows = state.astype(BF16)
        row = lax.broadcasted_iota(jnp.int32, (HEAD_ROWS, width), 0)
        top = jnp.where(row == 1, role, counts[held]).astype(F32).astype(BF16)
        both[role, :slots] = rows
        both[role, slots:] = top
        single[:slots] = rows
        single[slots:] = top


def pack(features, counts, ready):
    bins, slots, width = features.shape
    tall = slots + HEAD_ROWS
    outs = [
        shape((bins, tall, width), BF16),
        shape((tall, width), BF16),
        shape((tall, width), BF16),
        shape((bins, slots, width), F32),
    ]
    return call(pack_body, outs, [VMEM, SMEM, VMEM])(features, counts, ready)


def score_keys(keys, biases, width):
    bias = jnp.concatenate(biases, axis=0)
    return [
        jnp.concatenate([keys[:, at : at + 128], bias], axis=1) for at in range(0, width, 128)
    ]


def pick(array, places, slots, axis):
    parts = [lax.slice_in_dim(array, p * slots, (p + 1) * slots, axis=axis) for p in places]
    return jnp.concatenate(parts, axis=axis)


def early(own, near, query_weight, key_weight, value_weight, outs):
    turned_values, masks, powers, peaks, sums = outs
    width = own.shape[-1]
    slots = own.shape[1] - HEAD_ROWS
    head_size = width // HEADS
    per_group = HEADS * 128 // width
    factor = head_size ** (-0.5) * LOG2E
    blocks = [own[0], own[1]] + [h[role] for role in range(ROLES) for h in near]
    rows = jnp.concatenate([b[:slots] for b in blocks], axis=0)
    biases = [live_rows(b, slots) for b in blocks]
    queries = dot(rows[: ROLES * slots], query_weight[...]).astype(BF16)
    keys = dot(rows, key_weight[...]).astype(BF16)
    lane = lax.broadcasted_iota(jnp.int32, (slots, 128), 1)
    mark = jnp.where(lane == 0, 1.0, 0.0).astype(BF16)
    places = [
        [0, 1] + [2 + role * len(near) + n for n in range(len(near))] for role in range(ROLES)
    ]
    for role in range(ROLES):
        part = score_keys(
            pick(keys, places[role], slots, 0), [biases[p] for p in places[role]], width
        )
        for pair in range(HEADS // 2):
            masked = []
            for head in (2 * pair, 2 * pair + 1):
                group, inner = divmod(head, per_group)
                query = queries[role * slots : (role + 1) * slots]
                query = query[:, group * 128 : (group + 1) * 128]
                inside = (lane >= inner * head_size) & (lane < (inner + 1) * head_size)
                query = jnp.where(inside, query.astype(F32), 0.0).astype(BF16)
                masked.append(jnp.concatenate([query, mark], axis=1))
            masked = jnp.concatenate(masked, axis=0)
            at = role * (HEADS // 2) + pair
            masks[at] = masked
            scores = dot(part[2 * pair // per_group], masked, ROWS)
            peak = jnp.max(scores, axis=0, keepdims=True)
            power = jnp.exp2((scores - peak) * factor)
            powers[at] = power
            peaks[at] = peak
            sums[at] = jnp.sum(power, axis=0, keepdims=True)
    values = dot(value_weight[...], rows, COLUMNS).astype(BF16)
    for role in range(ROLES):
        turned_values[role] = pick(values, places[role], slots, 1)


def early_shapes(slots, width, near):
    keys = (2 + near) * slots
    pairs = ROLES * HEADS // 2
    return [
        shape((ROLES, width, keys), BF16),
        shape((pairs, 2 * slots, 256), BF16),
        shape((pairs, keys, 2 * slots), F32),
        shape((pairs, 1, 2 * slots), F32),
        shape((pairs, 1, 2 * slots), F32),
    ]


def run_early(own, near, weights):
    slots, width = own.shape[1] - HEAD_ROWS, own.shape[2]

    def body(own, *refs):
        n = len(near)
        early(own, refs[:n], *refs[n : n + 3], refs[n + 3 :])

    outs = early_shapes(slots, width, len(near))
    return call(body, outs, [VMEM] * (4 + len(near)))(own, *near, *weights[:3])


def late(residual, own, far, sides, flags, prior, weights, gains):
    turned_own, masks, powers, peaks, sums = prior
    _, key_weight, value_weight, out_weight, up_weight, down_weight = weights
    attention_gain, feed_gain = gains
    slots, width = residual.shape[1:]
    head_size = width // HEADS
    per_group = HEADS * 128 // width
    factor = head_size ** (-0.5) * LOG2E
    blocks, biases = [], []
    for role in range(ROLES):
        near = [(h[role], flag) for h, flag in far] + [(sides[role][...], flags[role])]
        for block, flag in near:
            blocks.append(block[:slots])
            biases.append(live_rows(block, slots, flag))
    count = len(blocks) // ROLES
    rows = jnp.concatenate(blocks, axis=0)
    keys = dot(rows, key_weight[...]).astype(BF16)
    values = dot(value_weight[...], rows, COLUMNS).astype(BF16)
    attended = []
    for role in range(ROLES):
        span = slice(role * count * slots, (role + 1) * count * slots)
        part = score_keys(keys[span], biases[role * count : (role + 1) * count], width)
        pieces = []
        for pair in range(HEADS // 2):
            at = role * (HEADS // 2) + pair
            scores = dot(part[2 * pair // per_group], masks[at], ROWS)
            before = peaks[at]
            peak = jnp.maximum(jnp.max(scores, axis=0, keepdims=True), before)
            power = jnp.exp2((scores - peak) * factor)
            rescale = jnp.exp2((before - peak) * factor)
            total = jnp.sum(power, axis=0, keepdims=True) + sums[at] * rescale
            inverse = 1.0 / total
            feature = slice(2 * pair * head_size, 2 * (pair + 1) * head_size)
            mixed = dot(values[feature, span], (power * inverse).astype(BF16)) + dot(
                turned_own[role, feature], (powers[at] * (rescale * inverse)).astype(BF16)
            )
            pieces += [mixed[:head_size, :slots], mixed[head_size:, slots:]]
        attended.append(jnp.concatenate(pieces, axis=0).astype(BF16))
    mixed = jnp.concatenate([dot(a, out_weight[...], TURNED) for a in attended], axis=0)
    state = jnp.concatenate([residual[0], residual[1]], axis=0)
    hidden = layer_norm(state + mixed, attention_gain[...])
    inner = jax.nn.gelu(dot(hidden.astype(BF16), up_weight[...])).astype(BF16)
    result = layer_norm(hidden + dot(inner, down_weight[...]), feed_gain[...])
    row = lax.broadcasted_iota(jnp.int32, (slots, width), 0).astype(F32)
    results = []
    for role in range(ROLES):
        live = row < own[role, slots : slots + 1, :].astype(F32)
        results.append(jnp.where(live, result[role * slots : (role + 1) * slots], 0.0))
    return results


def travel_body(results, own, places, spans, travel, stayed):
    slots, width = stayed.shape
    parity = lax.axis_index("gy") % 2
    span_z = spans[1]
    line = lax.broadcasted_iota(jnp.int32, (HEAD_ROWS, width), 0)
    for role in range(ROLES):
        place = places[1 - parity if role == 0 else parity]
        stays = place % span_z == lax.axis_index("gz")
        new_role = jnp.where((place // span_z) % 2 == parity, 1, 0)
        slot = jnp.where(stays, 1, 0)
        travel[slot, :slots] = results[role].astype(BF16)
        top = own[role, slots:].astype(F32)
        travel[slot, slots:] = jnp.where(line == 1, new_role.astype(F32), top).astype(BF16)

        @pl.when(stays)
        def _():
            stayed[...] = results[role]


def run_late(end, spans, residual, own, far, sides, around, prior, weights, gains, places=None):
    bins, slots, width = residual.shape
    tall = slots + HEAD_ROWS
    halos = [block for block, _ in far]
    args = [residual, own, *halos, *sides, *prior, *weights, *gains]
    specs = [VMEM] * len(args)
    if end == "bins":
        outs = [shape((bins, slots, width), F32)]
    else:
        outs = [shape((bins, tall, width), BF16), shape((slots, width), F32)]
        args.append(places)
        specs.append(SMEM)

    def inside(axis):
        if not around:
            return None
        index = lax.axis_index(axis)
        return (index > 0) & (index < lax.axis_size(axis) - 1)

    def body(*refs):
        ins, results = list(refs[: len(args)]), refs[len(args) :]

        def take(count):
            taken = ins[:count]
            del ins[:count]
            return taken

        residual, own = take(2)
        blocks = take(len(halos))
        flagged = [
            (block, inside(axis) if axis else None) for block, (_, axis) in zip(blocks, far)
        ]
        side_refs = take(2)
        flags = (None, inside("gy"))
        prior_refs, weight_refs, gain_refs = take(5), take(6), take(2)
        rows = late(
            residual, own, flagged, side_refs, flags, prior_refs, weight_refs, gain_refs
        )
        if end == "bins":
            (out,) = results
            parity = lax.axis_index("gy") % 2
            out[1 - parity] = rows[0]
            out[parity] = rows[1]
        else:
            travel_body(rows, own, ins[0], spans, *results)

    return call(body, outs, specs)(*args)


def choose(role, yes, no):
    return jnp.where(role < 0.5, yes.astype(F32), no.astype(F32))


def settle_body(travel, arrived, stayed, both, first, second, beside, residual):
    slots = stayed.shape[0]
    stay, came = travel[1], arrived[0]
    role = stay[slots + 1 : slots + 2].astype(F32)
    for index, single in ((0, first), (1, second)):
        block = choose(role, *((stay, came) if index == 0 else (came, stay))).astype(BF16)
        both[index] = block
        single[...] = block
        rows = stayed[...], came[:slots]
        residual[index] = choose(role, *(rows if index == 0 else rows[::-1]))
    peer, left = arrived[1], travel[0]
    role = peer[slots + 1 : slots + 2].astype(F32)
    beside[0] = choose(role, peer, left).astype(BF16)
    beside[1] = choose(role, left, peer).astype(BF16)


def settle(travel, arrived, stayed):
    bins, tall, width = travel.shape
    slots = stayed.shape[0]
    outs = [
        shape((bins, tall, width), BF16),
        shape((tall, width), BF16),
        shape((tall, width), BF16),
        shape((bins, tall, width), BF16),
        shape((bins, slots, width), F32),
    ]
    return call(settle_body, outs, [VMEM] * 3)(travel, arrived, stayed)


def relocate(state, counts, dest_bin, bins_y):
    total, slots, width = state.shape
    depth = lax.axis_size("gz")
    targets = dest_bin.reshape(-1)
    peer = targets % depth
    local = targets // depth % bins_y
    order = jnp.arange(total, dtype=jnp.int32)
    earlier = (peer[None, :] == peer[:, None]) & (order[None, :] < order[:, None])
    slot = jnp.sum(earlier.astype(jnp.int32), axis=1)
    capacity = (total + depth - 1) // depth
    outgoing = jnp.zeros((depth, capacity, slots, width), F32).at[peer, slot].set(state)
    outgoing_counts = jnp.zeros((depth, capacity), jnp.int32).at[peer, slot].set(counts)
    outgoing_places = jnp.full((depth, capacity), total, jnp.int32).at[peer, slot].set(local)
    arrived = lax.all_to_all(outgoing.astype(BF16), "gz", 0, 0, tiled=True).astype(F32)
    arrived_counts = lax.all_to_all(outgoing_counts, "gz", 0, 0, tiled=True)
    places = lax.all_to_all(outgoing_places, "gz", 0, 0, tiled=True).reshape(-1)
    moved = jnp.zeros((total, slots, width), F32)
    moved = moved.at[places].set(arrived.reshape(-1, slots, width), mode="drop")
    moved_counts = jnp.zeros((total,), jnp.int32)
    moved_counts = moved_counts.at[places].set(arrived_counts.reshape(-1), mode="drop")
    return moved, moved_counts


def exchange(own, first, second, axes, around):
    far = []
    for axis in axes:
        count = lax.axis_size(axis)
        for parity in range(2):
            pairs = swaps(count, parity, around)
            if not pairs:
                continue
            block = lax.ppermute(own, axis, pairs)
            far.append((block, axis if around and parity == 1 else None))
    sides = []
    for parity, block in ((0, first), (1, second)):
        sides.append(
            lax.ppermute(block, "gy", swaps(lax.axis_size("gy"), parity, around))
        )
    return far, sides


def shards(features, occupancy, dest_bin, *rest):
    weights, gains = rest[:6], [g.reshape(1, -1) for g in rest[6:]]
    slots, width = features.shape[3:]
    state = features.reshape(2, slots, width)
    counts = occupancy.reshape(2)
    places = dest_bin.reshape(2)
    depth = lax.axis_size("gz")
    spans = (2 * lax.axis_size("gy"), depth)

    ready = prepare(slots, width)
    own, first, second, residual = pack(state, counts, ready)
    far, sides = exchange(own, first, second, ("gx", "gz"), True)
    prior = run_early(own, [], weights)
    end = "travel" if depth == 2 else "bins"
    results = run_late(
        end, spans, residual, own, far, sides, True, prior, weights, gains,
        places if depth == 2 else None,
    )
    if depth == 2:
        travel, stayed = results
        arrived = lax.ppermute(travel, "gz", swaps(depth, 0))
        own, first, second, beside, residual = settle(travel, arrived, stayed)
        near, axes = [beside], ("gx",)
    else:
        state, counts = relocate(results[0], counts, places, 2)
        own, first, second, residual = pack(state, counts, ready)
        near, axes = [], ("gx", "gz")
    far, sides = exchange(own, first, second, axes, False)
    prior = run_early(own, near, weights)
    (out,) = run_late(
        "bins", spans, residual, own, far, sides, False, prior, weights, gains
    )
    return out.reshape(features.shape)


def solution(mesh):
    placed = (
        P("gx", "gy", "gz", None, None),
        P("gx", "gy", "gz"),
        P("gx", "gy", "gz"),
        *([P()] * 8),
    )
    return jax.shard_map(
        shards,
        mesh=mesh,
        in_specs=placed,
        out_specs=P("gx", "gy", "gz", None, None),
        check_vma=False,
    )
```

```python
import math

import jax
import jax.numpy as jnp
import numpy as np
from jax import lax
from jax.experimental import pallas as pl
from jax.experimental.pallas import tpu as pltpu
from jax.sharding import PartitionSpec as P

HEADS = 8
EPSILON = 1e-05
LOG2E = 1.4426950408889634
DEAD = -1e30
HEAD_ROWS = 16
ROLES = 2
ENDS = ((None, 'ring'), (None, 'ring'))

F32 = jnp.float32
BF16 = jnp.bfloat16

VMEM = pl.BlockSpec(memory_space=pltpu.VMEM)
ROWS = (((1,), (1,)), ((), ()))
COLUMNS = (((0,), (1,)), ((), ()))
TURNED = (((0,), (0,)), ((), ()))


def shape(dims, dtype):
    return jax.ShapeDtypeStruct(dims, dtype)


def call(body, outs, specs, scratch=(), limit=30 << 20):
    return pl.pallas_call(
        body,
        out_shape=outs,
        in_specs=specs,
        out_specs=jax.tree.map(lambda _: VMEM, outs),
        scratch_shapes=scratch,
        compiler_params=pltpu.CompilerParams(vmem_limit_bytes=limit),
    )


def swaps(count, parity):
    pairs = []
    for low in range(parity, count - 1, 2):
        pairs += [(low, low + 1), (low + 1, low)]
    return pairs


def swap(block, axis, parity, ends):
    count = lax.axis_size(axis)
    pairs = swaps(count, parity)
    if parity == 1 and count % 2 == 0 and count > 2:
        if ends == "ring":
            pairs += [(0, count - 1), (count - 1, 0)]
        if ends == "peer" and lax.axis_size("gz") == 2:
            names = ("gx", "gy", "gz")
            sizes = [lax.axis_size(n) for n in names]
            grid = np.arange(math.prod(sizes)).reshape(sizes)
            along = np.moveaxis(grid, names.index(axis), 0)
            outer = along[[0, -1]]
            pairs = [
                (int(i), int(j)) for a, b in pairs for i, j in zip(along[a].flat, along[b].flat)
            ]
            pairs += [(int(i), int(j)) for i, j in zip(outer.flat, outer[..., ::-1].flat)]
            axis = names
    return lax.ppermute(block, axis, pairs)


def dot(a, b, dims=(((1,), (0,)), ((), ()))):
    return lax.dot_general(a, b, dims, preferred_element_type=F32)


def layer_norm(values, gain):
    centre = values - jnp.mean(values, axis=-1, keepdims=True)
    spread = jnp.mean(centre * centre, axis=-1, keepdims=True)
    return centre * lax.rsqrt(spread + EPSILON) * gain


def live_rows(block, slots, present=None):
    count = block[slots : slots + 1, :128].astype(F32)
    if present is not None:
        count = jnp.where(present, count, 0.0)
    row = lax.broadcasted_iota(jnp.int32, (slots, 128), 0).astype(F32)
    return jnp.where(row < count, 0.0, DEAD).astype(BF16)


def prepare_body(out):
    out[...] = jnp.zeros_like(out)


def prepare(slots, width):
    return pl.pallas_call(
        prepare_body,
        out_shape=shape((8, 128), F32),
        out_specs=VMEM,
        compiler_params=pltpu.CompilerParams(vmem_limit_bytes=1 << 20),
        cost_estimate=pl.CostEstimate(
            flops=80000 * slots * width, transcendentals=0, bytes_accessed=0
        ),
        name="prepare",
    )()


def entry(pair, index):
    return jnp.where(index == 0, pair[:, 0:1], pair[:, 1:2])


def scalar(block):
    return jnp.sum(block.astype(F32)).astype(jnp.int32)


def pack_body(features, counts, ready, both, first, second, residual):
    slots, width = features.shape[1:]
    parity = lax.axis_index("gy") % 2
    del ready
    for role, single in ((0, first), (1, second)):
        held = 1 - parity if role == 0 else parity
        state = features[held]
        residual[role] = state
        rows = state.astype(BF16)
        row = lax.broadcasted_iota(jnp.int32, (HEAD_ROWS, width), 0)
        top = jnp.where(row == 1, role, entry(counts[...], held)).astype(F32).astype(BF16)
        both[role, :slots] = rows
        both[role, slots:] = top
        single[:slots] = rows
        single[slots:] = top


def pack(features, counts, ready):
    bins, slots, width = features.shape
    tall = slots + HEAD_ROWS
    outs = [
        shape((bins, tall, width), BF16),
        shape((tall, width), BF16),
        shape((tall, width), BF16),
        shape((bins, slots, width), F32),
    ]
    return call(pack_body, outs, [VMEM] * 3)(
        features, counts.reshape(1, bins), ready
    )


def score_keys(keys, biases, width):
    bias = jnp.concatenate(biases, axis=0)
    return [
        jnp.concatenate([keys[:, at : at + 128], bias], axis=1) for at in range(0, width, 128)
    ]


def pick(array, places, slots, axis):
    parts = [lax.slice_in_dim(array, p * slots, (p + 1) * slots, axis=axis) for p in places]
    return jnp.concatenate(parts, axis=axis)


def scores_part(part, pair, per_group, mask, outs, at, factor):
    powers, peaks, sums = outs
    scores = dot(part[2 * pair // per_group], mask, ROWS)
    peak = jnp.max(scores, axis=0, keepdims=True)
    power = jnp.exp2((scores - peak) * factor)
    powers[at] = power
    peaks[at] = peak
    sums[at] = jnp.sum(power, axis=0, keepdims=True)


def constants(width):
    head_size = width // HEADS
    return head_size, HEADS * 128 // width, head_size ** (-0.5) * LOG2E


def early_body(own, near, weights, outs):
    query_weight, key_weight, value_weight = weights
    masks, turned_values, *parts = outs
    width = own.shape[-1]
    slots = own.shape[1] - HEAD_ROWS
    head_size, per_group, factor = constants(width)
    blocks = [own[0], own[1], *near]
    rows = jnp.concatenate([b[:slots] for b in blocks], axis=0)
    biases = [live_rows(b, slots) for b in blocks]
    queries = dot(rows[: ROLES * slots], query_weight[...]).astype(BF16)
    keys = dot(rows, key_weight[...]).astype(BF16)
    lane = lax.broadcasted_iota(jnp.int32, (slots, 128), 1)
    mark = jnp.where(lane == 0, 1.0, 0.0).astype(BF16)
    places = [[0, 1] + ([2 + role] if near else []) for role in range(ROLES)]
    for role in range(ROLES):
        part = score_keys(
            pick(keys, places[role], slots, 0), [biases[p] for p in places[role]], width
        )
        for pair in range(HEADS // 2):
            masked = []
            for head in (2 * pair, 2 * pair + 1):
                group, inner = divmod(head, per_group)
                query = queries[role * slots : (role + 1) * slots]
                query = query[:, group * 128 : (group + 1) * 128]
                inside = (lane >= inner * head_size) & (lane < (inner + 1) * head_size)
                query = jnp.where(inside, query.astype(F32), 0.0).astype(BF16)
                masked.append(jnp.concatenate([query, mark], axis=1))
            masked = jnp.concatenate(masked, axis=0)
            at = role * (HEADS // 2) + pair
            masks[at] = masked
            scores_part(part, pair, per_group, masked, parts, at, factor)
    values = dot(value_weight[...], rows, COLUMNS).astype(BF16)
    for role in range(ROLES):
        turned_values[role] = pick(values, places[role], slots, 1)


def part_shapes(slots, width, blocks):
    keys = blocks * slots
    pairs = ROLES * HEADS // 2
    return [
        shape((ROLES, width, keys), BF16),
        shape((pairs, keys, 2 * slots), F32),
        shape((pairs, 1, 2 * slots), F32),
        shape((pairs, 1, 2 * slots), F32),
    ]


def run_early(own, beside, weights):
    slots, width = own.shape[1] - HEAD_ROWS, own.shape[2]

    def body(own, *refs):
        near = []
        if beside:
            peer, left = refs[0][...], refs[1][...]
            role = peer[slots + 1 : slots + 2].astype(F32)
            near = [choose(role, peer, left).astype(BF16), choose(role, left, peer).astype(BF16)]
        n = len(beside)
        early_body(own, near, refs[n : n + 3], refs[n + 3 :])

    outs = part_shapes(slots, width, 3 if beside else 2)
    outs = [shape((ROLES * HEADS // 2, 2 * slots, 256), BF16)] + outs
    args = [own, *beside, *weights[:3]]
    masks, *part = call(body, outs, [VMEM] * len(args))(*args)
    return masks, part


def run_middle(far, masks, weights, around):
    slots, width = far[0][0].shape[1] - HEAD_ROWS, far[0][0].shape[2]
    n = len(far)
    _, per_group, factor = constants(width)

    def body(*refs):
        halos, (masks, key_weight, value_weight), outs = refs[:n], refs[n : n + 3], refs[n + 3 :]
        turned_values, *parts = outs
        blocks, biases = [], []
        for role in range(ROLES):
            for halo, (_, axis) in zip(halos, far):
                block = halo[role]
                blocks.append(block[:slots])
                biases.append(live_rows(block, slots, inside(axis, around)))
        rows = jnp.concatenate(blocks, axis=0)
        keys = dot(rows, key_weight[...]).astype(BF16)
        for role in range(ROLES):
            span = slice(role * n * slots, (role + 1) * n * slots)
            part = score_keys(keys[span], biases[role * n : (role + 1) * n], width)
            for pair in range(HEADS // 2):
                at = role * (HEADS // 2) + pair
                scores_part(part, pair, per_group, masks[at], parts, at, factor)
        values = dot(value_weight[...], rows, COLUMNS).astype(BF16)
        for role in range(ROLES):
            turned_values[role] = values[:, role * n * slots : (role + 1) * n * slots]

    args = [block for block, _ in far] + [masks, weights[1], weights[2]]
    return call(body, part_shapes(slots, width, n), [VMEM] * len(args))(*args)


def inside(axis, around):
    if axis is None or not around:
        return None
    index = lax.axis_index(axis)
    return (index > 0) & (index < lax.axis_size(axis) - 1)


def attend_role(role, block, flag, masks, parts, key_weight, value_weight):
    width = block.shape[1]
    slots = block.shape[0] - HEAD_ROWS
    head_size, per_group, factor = constants(width)
    rows = block[:slots]
    keys = score_keys(
        dot(rows, key_weight[...]).astype(BF16), [live_rows(block, slots, flag)], width
    )
    values = dot(value_weight[...], rows, COLUMNS).astype(BF16)
    pieces = []
    for pair in range(HEADS // 2):
        at = role * (HEADS // 2) + pair
        scores = dot(keys[2 * pair // per_group], masks[at], ROWS)
        peak = jnp.max(scores, axis=0, keepdims=True)
        for _, _, peaks, _ in parts:
            peak = jnp.maximum(peak, peaks[at])
        power = jnp.exp2((scores - peak) * factor)
        total = jnp.sum(power, axis=0, keepdims=True)
        rescales = []
        for _, _, peaks, sums in parts:
            rescales.append(jnp.exp2((peaks[at] - peak) * factor))
            total = total + sums[at] * rescales[-1]
        inverse = 1.0 / total
        feature = slice(2 * pair * head_size, 2 * (pair + 1) * head_size)
        mixed = dot(values[feature], (power * inverse).astype(BF16))
        for (turned, powers, _, _), rescale in zip(parts, rescales):
            weights = (powers[at] * (rescale * inverse)).astype(BF16)
            mixed = mixed + dot(turned[role, feature], weights)
        pieces += [mixed[:head_size, :slots], mixed[head_size:, slots:]]
    return jnp.concatenate(pieces, axis=0).astype(BF16)


def update(state, attended, out_weight, up_weight, down_weight, attention_gain, feed_gain):
    mixed = jnp.concatenate([dot(a, out_weight[...], TURNED) for a in attended], axis=0)
    hidden = layer_norm(state + mixed, attention_gain[...])
    inner = jax.nn.gelu(dot(hidden.astype(BF16), up_weight[...])).astype(BF16)
    return layer_norm(hidden + dot(inner, down_weight[...]), feed_gain[...])


def keep_live(result, top):
    row = lax.broadcasted_iota(jnp.int32, result.shape, 0).astype(F32)
    return jnp.where(row < top, result, 0.0)


def run_bins(residual, own, sides, around, masks, parts, weights, gains):
    bins, slots, width = residual.shape
    args = [residual, own, *sides, masks, *parts[0], *parts[1], *weights[1:], *gains]

    def body(residual, own, first, second, masks, *refs):
        parts, refs = (refs[:4], refs[4:8]), refs[8:]
        key_weight, value_weight, *rest, out = refs
        attended = [
            attend_role(role, side[...], flag, masks, parts, key_weight, value_weight)
            for role, side, flag in ((0, first, None), (1, second, inside("gy", around)))
        ]
        state = jnp.concatenate([residual[0], residual[1]], axis=0)
        result = update(state, attended, *rest)
        parity = lax.axis_index("gy") % 2
        for role in range(ROLES):
            rows = result[role * slots : (role + 1) * slots]
            rows = keep_live(rows, own[role, slots : slots + 1, :].astype(F32))
            out[1 - parity if role == 0 else parity] = rows

    outs = shape((bins, slots, width), F32)
    return call(body, outs, [VMEM] * len(args))(*args)


def run_one(leaving, spans, residual, own, sides, around, masks, parts, weights, gains, places):
    _, slots, width = residual.shape
    tall = slots + HEAD_ROWS
    args = [places, residual, own, *sides, masks, *parts[0], *parts[1], *weights[1:], *gains]

    def body(places, residual, own, first, second, masks, *refs):
        parts, refs = (refs[:4], refs[4:8]), refs[8:]
        key_weight, value_weight, *rest = refs[:7]
        outs = refs[7:]
        parity = lax.axis_index("gy") % 2
        stays = scalar(entry(places[...], 1 - parity)) % spans[1] == lax.axis_index("gz")
        role = jnp.where(stays, 1, 0) if leaving else jnp.where(stays, 0, 1)
        place = scalar(entry(places[...], jnp.where(role == 0, 1 - parity, parity)))
        new_role = jnp.where((place // spans[1]) % 2 == parity, 1, 0)
        ahead = role == 0
        block = jnp.where(ahead, first[...].astype(F32), second[...].astype(F32)).astype(BF16)
        flag = inside("gy", around)
        flag = flag if flag is None else ahead | flag
        attended = attend_role(role, block, flag, masks, parts, key_weight, value_weight)
        result = update(residual[role], [attended], *rest)
        top = own[role, slots:].astype(F32)
        result = keep_live(result, top[:1])
        line = lax.broadcasted_iota(jnp.int32, (HEAD_ROWS, width), 0)
        outs[0][:slots] = result.astype(BF16)
        outs[0][slots:] = jnp.where(line == 1, new_role.astype(F32), top).astype(BF16)
        if not leaving:
            outs[1][...] = result

    outs = [shape((tall, width), BF16)]
    if not leaving:
        outs.append(shape((slots, width), F32))
    args[0] = places.reshape(1, -1)
    return call(body, outs, [VMEM] * len(args))(*args)


def choose(role, yes, no):
    return jnp.where(role < 0.5, yes.astype(F32), no.astype(F32))


def settle_body(stay, stayed, came, both, first, second, residual):
    slots = stayed.shape[0]
    stay, came = stay[...], came[...]
    role = stay[slots + 1 : slots + 2].astype(F32)
    for index, single in ((0, first), (1, second)):
        block = choose(role, *((stay, came) if index == 0 else (came, stay))).astype(BF16)
        both[index] = block
        single[...] = block
        rows = stayed[...], came[:slots]
        residual[index] = choose(role, *(rows if index == 0 else rows[::-1]))


def settle(stay, stayed, came):
    slots, width = stayed.shape
    tall = slots + HEAD_ROWS
    outs = [
        shape((ROLES, tall, width), BF16),
        shape((tall, width), BF16),
        shape((tall, width), BF16),
        shape((ROLES, slots, width), F32),
    ]
    return call(settle_body, outs, [VMEM] * 3)(stay, stayed, came)


def relocate(state, counts, dest_bin, bins_y):
    total, slots, width = state.shape
    depth = lax.axis_size("gz")
    targets = dest_bin.reshape(-1)
    peer = targets % depth
    local = targets // depth % bins_y
    order = jnp.arange(total, dtype=jnp.int32)
    earlier = (peer[None, :] == peer[:, None]) & (order[None, :] < order[:, None])
    slot = jnp.sum(earlier.astype(jnp.int32), axis=1)
    capacity = (total + depth - 1) // depth
    outgoing = jnp.zeros((depth, capacity, slots, width), F32).at[peer, slot].set(state)
    outgoing_counts = jnp.zeros((depth, capacity), jnp.int32).at[peer, slot].set(counts)
    outgoing_places = jnp.full((depth, capacity), total, jnp.int32).at[peer, slot].set(local)
    arrived = lax.all_to_all(outgoing.astype(BF16), "gz", 0, 0, tiled=True).astype(F32)
    arrived_counts = lax.all_to_all(outgoing_counts, "gz", 0, 0, tiled=True)
    places = lax.all_to_all(outgoing_places, "gz", 0, 0, tiled=True).reshape(-1)
    moved = jnp.zeros((total, slots, width), F32)
    moved = moved.at[places].set(arrived.reshape(-1, slots, width), mode="drop")
    moved_counts = jnp.zeros((total,), jnp.int32)
    moved_counts = moved_counts.at[places].set(arrived_counts.reshape(-1), mode="drop")
    return moved, moved_counts


def exchange(own, first, second, axes, ends):
    far = []
    for axis in axes:
        for parity in range(2):
            if not swaps(lax.axis_size(axis), parity):
                continue
            how = ends[0] if axis == "gx" else None
            block = swap(own, axis, parity, how)
            far.append((block, axis if how and parity == 1 else None))
    sides = []
    for parity, block in ((0, first), (1, second)):
        sides.append(swap(block, "gy", parity, ends[1]))
    return far, sides


def shards(features, occupancy, dest_bin, *rest):
    weights, gains = rest[:6], [g.reshape(1, -1) for g in rest[6:]]
    slots, width = features.shape[3:]
    state = features.reshape(2, slots, width)
    counts = occupancy.reshape(2)
    places = dest_bin.reshape(2)
    depth = lax.axis_size("gz")
    spans = (2 * lax.axis_size("gy"), depth)

    def finish(own, residual, beside, far, sides, ends):
        around = bool(ends[1])
        masks, first = run_early(own, beside, weights)
        second = run_middle(far, masks, weights, True)
        return residual, own, sides, around, masks, (first, second), weights, gains

    ready = prepare(slots, width)
    own, first, second, residual = pack(state, counts, ready)
    far, sides = exchange(own, first, second, ("gx", "gz"), ENDS[0])
    known = finish(own, residual, [], far, sides, ENDS[0])
    if depth == 2:
        (leave,) = run_one(True, spans, *known, places)
        came = swap(leave, "gz", 0, None)
        stay, stayed = run_one(False, spans, *known, places)
        peer = swap(stay, "gz", 0, None)
        own, first, second, residual = settle(stay, stayed, came)
        beside, axes = [peer, leave], ("gx",)
    else:
        state = run_bins(*known)
    if depth != 2:
        state, counts = relocate(state, counts, places, 2)
        own, first, second, residual = pack(state, counts, ready)
        beside, axes = [], ("gx", "gz")
    far, sides = exchange(own, first, second, axes, ENDS[1])
    out = run_bins(*finish(own, residual, beside, far, sides, ENDS[1]))
    return out.reshape(features.shape)


def solution(mesh):
    placed = (
        P("gx", "gy", "gz", None, None),
        P("gx", "gy", "gz"),
        P("gx", "gy", "gz"),
        *([P()] * 8),
    )
    return jax.shard_map(
        shards,
        mesh=mesh,
        in_specs=placed,
        out_specs=P("gx", "gy", "gz", None, None),
        check_vma=False,
    )
```

```python
import math

import jax
import jax.numpy as jnp
import numpy as np
from jax import lax
from jax.experimental import pallas as pl
from jax.experimental.pallas import tpu as pltpu
from jax.sharding import PartitionSpec as P

HEADS = 8
EPSILON = 1e-05
LOG2E = 1.4426950408889634
DEAD = -1e30
HEAD_ROWS = 16
ROLES = 2
X0, X1, Y0, Y1, Z0, Z1 = [(axis, parity) for axis in ("gx", "gy", "gz") for parity in (0, 1)]
ORDERS = ((X0, X1, Z0, Z1, Y0, Y1), (X0, X1, Z0, Z1, Y0, Y1))
LAST = ((X1, Z0, Z1), (X1,))
ENDS = ((None, 'ring'), (None, 'ring'))

F32 = jnp.float32
BF16 = jnp.bfloat16

VMEM = pl.BlockSpec(memory_space=pltpu.VMEM)
ROWS = (((1,), (1,)), ((), ()))
COLUMNS = (((0,), (1,)), ((), ()))
TURNED = (((0,), (0,)), ((), ()))


def shape(dims, dtype):
    return jax.ShapeDtypeStruct(dims, dtype)


def call(body, outs, specs, scratch=(), out_specs=None, limit=30 << 20):
    return pl.pallas_call(
        body,
        out_shape=outs,
        in_specs=specs,
        out_specs=out_specs or jax.tree.map(lambda _: VMEM, outs),
        scratch_shapes=scratch,
        compiler_params=pltpu.CompilerParams(vmem_limit_bytes=limit),
    )


def swaps(count, parity):
    pairs = []
    for low in range(parity, count - 1, 2):
        pairs += [(low, low + 1), (low + 1, low)]
    return pairs


def swap(block, axis, parity, ends):
    count = lax.axis_size(axis)
    pairs = swaps(count, parity)
    if parity == 1 and count % 2 == 0 and count > 2:
        if ends == "ring":
            pairs += [(0, count - 1), (count - 1, 0)]
        if ends == "peer" and lax.axis_size("gz") == 2:
            names = ("gx", "gy", "gz")
            sizes = [lax.axis_size(n) for n in names]
            grid = np.arange(math.prod(sizes)).reshape(sizes)
            along = np.moveaxis(grid, names.index(axis), 0)
            outer = along[[0, -1]]
            pairs = [
                (int(i), int(j)) for a, b in pairs for i, j in zip(along[a].flat, along[b].flat)
            ]
            pairs += [(int(i), int(j)) for i, j in zip(outer.flat, outer[..., ::-1].flat)]
            axis = names
    return lax.ppermute(block, axis, pairs)


def dot(a, b, dims=(((1,), (0,)), ((), ()))):
    return lax.dot_general(a, b, dims, preferred_element_type=F32)


def layer_norm(values, gain):
    centre = values - jnp.mean(values, axis=-1, keepdims=True)
    spread = jnp.mean(centre * centre, axis=-1, keepdims=True)
    return centre * lax.rsqrt(spread + EPSILON) * gain


def live_rows(block, slots, present=None):
    count = block[slots : slots + 1, :128].astype(F32)
    if present is not None:
        count = jnp.where(present, count, 0.0)
    row = lax.broadcasted_iota(jnp.int32, (slots, 128), 0).astype(F32)
    return jnp.where(row < count, 0.0, DEAD).astype(BF16)


def prepare_body(out):
    out[...] = jnp.zeros_like(out)


def prepare(slots, width):
    return pl.pallas_call(
        prepare_body,
        out_shape=shape((8, 128), F32),
        out_specs=VMEM,
        compiler_params=pltpu.CompilerParams(vmem_limit_bytes=1 << 20),
        cost_estimate=pl.CostEstimate(
            flops=80000 * slots * width, transcendentals=0, bytes_accessed=0
        ),
        name="prepare",
    )()


def entry(pair, index):
    return jnp.where(index == 0, pair[:, 0:1], pair[:, 1:2])


def scalar(block):
    return jnp.sum(block.astype(F32)).astype(jnp.int32)


def pack_body(features, counts, ready, both, first, second, residual):
    slots, width = features.shape[1:]
    parity = lax.axis_index("gy") % 2
    del ready
    for role, single in ((0, first), (1, second)):
        held = 1 - parity if role == 0 else parity
        state = features[held]
        residual[role] = state
        rows = state.astype(BF16)
        row = lax.broadcasted_iota(jnp.int32, (HEAD_ROWS, width), 0)
        top = jnp.where(row == 1, role, entry(counts[...], held)).astype(F32).astype(BF16)
        both[role, :slots] = rows
        both[role, slots:] = top
        single[:slots] = rows
        single[slots:] = top


def pack(features, counts, ready):
    bins, slots, width = features.shape
    tall = slots + HEAD_ROWS
    outs = [
        shape((bins, tall, width), BF16),
        shape((tall, width), BF16),
        shape((tall, width), BF16),
        shape((bins, slots, width), F32),
    ]
    return call(pack_body, outs, [VMEM] * 3)(
        features, counts.reshape(1, bins), ready
    )


def score_keys(keys, biases, width):
    bias = jnp.concatenate(biases, axis=0)
    return [
        jnp.concatenate([keys[:, at : at + 128], bias], axis=1) for at in range(0, width, 128)
    ]


def pick(array, places, slots, axis):
    parts = [lax.slice_in_dim(array, p * slots, (p + 1) * slots, axis=axis) for p in places]
    return jnp.concatenate(parts, axis=axis)


def scores_part(part, pair, per_group, mask, outs, at, factor):
    powers, peaks, sums = outs
    scores = dot(part[2 * pair // per_group], mask, ROWS)
    peak = jnp.max(scores, axis=0, keepdims=True)
    power = jnp.exp2((scores - peak) * factor)
    powers[at] = power
    peaks[at] = peak
    sums[at] = jnp.sum(power, axis=0, keepdims=True)


def constants(width):
    head_size = width // HEADS
    return head_size, HEADS * 128 // width, head_size ** (-0.5) * LOG2E


def early_body(own, near, weights, outs):
    query_weight, key_weight, value_weight = weights
    masks, turned_values, *parts = outs
    width = own.shape[-1]
    slots = own.shape[1] - HEAD_ROWS
    head_size, per_group, factor = constants(width)
    blocks = [own[0], own[1], *near]
    rows = jnp.concatenate([b[:slots] for b in blocks], axis=0)
    biases = [live_rows(b, slots) for b in blocks]
    queries = dot(rows[: ROLES * slots], query_weight[...]).astype(BF16)
    keys = dot(rows, key_weight[...]).astype(BF16)
    lane = lax.broadcasted_iota(jnp.int32, (slots, 128), 1)
    mark = jnp.where(lane == 0, 1.0, 0.0).astype(BF16)
    places = [[0, 1] + ([2 + role] if near else []) for role in range(ROLES)]
    for role in range(ROLES):
        part = score_keys(
            pick(keys, places[role], slots, 0), [biases[p] for p in places[role]], width
        )
        for pair in range(HEADS // 2):
            masked = []
            for head in (2 * pair, 2 * pair + 1):
                group, inner = divmod(head, per_group)
                query = queries[role * slots : (role + 1) * slots]
                query = query[:, group * 128 : (group + 1) * 128]
                inside = (lane >= inner * head_size) & (lane < (inner + 1) * head_size)
                query = jnp.where(inside, query.astype(F32), 0.0).astype(BF16)
                masked.append(jnp.concatenate([query, mark], axis=1))
            masked = jnp.concatenate(masked, axis=0)
            at = role * (HEADS // 2) + pair
            masks[at] = masked
            scores_part(part, pair, per_group, masked, parts, at, factor)
    values = dot(value_weight[...], rows, COLUMNS).astype(BF16)
    for role in range(ROLES):
        turned_values[role] = pick(values, places[role], slots, 1)


def part_shapes(slots, width, blocks):
    keys = blocks * slots
    pairs = ROLES * HEADS // 2
    return [
        shape((ROLES, width, keys), BF16),
        shape((pairs, keys, 2 * slots), F32),
        shape((pairs, 1, 2 * slots), F32),
        shape((pairs, 1, 2 * slots), F32),
    ]


def run_early(own, beside, weights):
    slots, width = own.shape[1] - HEAD_ROWS, own.shape[2]

    def body(own, *refs):
        near = []
        if beside:
            peer, left = refs[0][...], refs[1][...]
            role = peer[slots + 1 : slots + 2].astype(F32)
            near = [choose(role, peer, left).astype(BF16), choose(role, left, peer).astype(BF16)]
        n = len(beside)
        early_body(own, near, refs[n : n + 3], refs[n + 3 :])

    outs = part_shapes(slots, width, 3 if beside else 2)
    outs = [shape((ROLES * HEADS // 2, 2 * slots, 256), BF16)] + outs
    args = [own, *beside, *weights[:3]]
    masks, *part = call(body, outs, [VMEM] * len(args))(*args)
    return masks, part


def run_middle(far, masks, weights, around):
    slots, width = far[0][0].shape[1] - HEAD_ROWS, far[0][0].shape[2]
    n = len(far)
    _, per_group, factor = constants(width)

    def body(*refs):
        halos, (masks, key_weight, value_weight), outs = refs[:n], refs[n : n + 3], refs[n + 3 :]
        turned_values, *parts = outs
        blocks, biases = [], []
        for role in range(ROLES):
            for halo, (_, axis) in zip(halos, far):
                block = halo[role]
                blocks.append(block[:slots])
                biases.append(live_rows(block, slots, inside(axis, around)))
        rows = jnp.concatenate(blocks, axis=0)
        keys = dot(rows, key_weight[...]).astype(BF16)
        for role in range(ROLES):
            span = slice(role * n * slots, (role + 1) * n * slots)
            part = score_keys(keys[span], biases[role * n : (role + 1) * n], width)
            for pair in range(HEADS // 2):
                at = role * (HEADS // 2) + pair
                scores_part(part, pair, per_group, masks[at], parts, at, factor)
        values = dot(value_weight[...], rows, COLUMNS).astype(BF16)
        for role in range(ROLES):
            turned_values[role] = values[:, role * n * slots : (role + 1) * n * slots]

    args = [block for block, _ in far] + [masks, weights[1], weights[2]]
    return call(body, part_shapes(slots, width, n), [VMEM] * len(args))(*args)


def inside(axis, around):
    if axis is None or not around:
        return None
    index = lax.axis_index(axis)
    return (index > 0) & (index < lax.axis_size(axis) - 1)


def attend_role(role, near, masks, parts, key_weight, value_weight, scratch):
    side_keys, side_values, turned = scratch
    width = near[0][0].shape[1]
    slots = near[0][0].shape[0] - HEAD_ROWS
    head_size, per_group, factor = constants(width)
    rows = jnp.concatenate([block[:slots] for block, _ in near], axis=0)
    biases = [live_rows(block, slots, flag) for block, flag in near]
    keys = score_keys(dot(rows, key_weight[...]).astype(BF16), biases, width)
    for group, key in enumerate(keys):
        side_keys[group] = key
    side_values[...] = dot(value_weight[...], rows, COLUMNS).astype(BF16)

    def step(pair):
        at = role * (HEADS // 2) + pair
        scores = dot(side_keys[2 * pair // per_group], masks[at], ROWS)
        peak = jnp.max(scores, axis=0, keepdims=True)
        for _, _, peaks, _ in parts:
            peak = jnp.maximum(peak, peaks[at])
        power = jnp.exp2((scores - peak) * factor)
        total = jnp.sum(power, axis=0, keepdims=True)
        rescales = []
        for _, _, peaks, sums in parts:
            rescales.append(jnp.exp2((peaks[at] - peak) * factor))
            total = total + sums[at] * rescales[-1]
        inverse = 1.0 / total
        feature = pl.ds(pl.multiple_of(2 * pair * head_size, 2 * head_size), 2 * head_size)
        mixed = dot(side_values[feature], (power * inverse).astype(BF16))
        for (turned_part, powers, _, _), rescale in zip(parts, rescales):
            weights = (powers[at] * (rescale * inverse)).astype(BF16)
            mixed = mixed + dot(turned_part[role, feature], weights)
        pieces = [mixed[:head_size, :slots], mixed[head_size:, slots:]]
        turned[feature] = jnp.concatenate(pieces, axis=0).astype(BF16)

    for pair in range(HEADS // 2):
        step(pair)
    return turned[...]


def gelu(x):
    half = 0.5 * x
    return half + half * jnp.tanh(x * (0.7978845608028654 + 0.035677408136300125 * (x * x)))


def update(state, attended, weights, gains):
    out_weight, up_weight, down_weight = weights
    attention_gain, feed_gain = gains
    mixed = dot(attended, out_weight[...], TURNED)
    hidden = layer_norm(state + mixed, attention_gain[...])
    narrow = hidden.astype(BF16)
    inner = gelu(dot(narrow, up_weight[...])).astype(BF16)
    return layer_norm(hidden + dot(inner, down_weight[...]), feed_gain[...])


def late_scratch(slots, width, blocks):
    return [
        pltpu.VMEM((width // 128, blocks * slots, 256), BF16),
        pltpu.VMEM((width, blocks * slots), BF16),
        pltpu.VMEM((width, slots), BF16),
    ]


def keep_live(result, top):
    row = lax.broadcasted_iota(jnp.int32, result.shape, 0).astype(F32)
    return jnp.where(row < top, result, 0.0)


def run_bins(residual, own, last, sides, around, masks, parts, weights, gains):
    bins, slots, width = residual.shape
    n = len(last)
    halos = [block for block, _ in last]
    args = [residual, own, *halos, *sides, masks, *parts[0], *parts[1], *weights[1:], *gains]

    def body(residual, own, *refs):
        halos, refs = refs[:n], refs[n:]
        sides, masks, refs = refs[:2], refs[2], refs[3:]
        parts, refs = (refs[:4], refs[4:8]), refs[8:]
        key_weight, value_weight = refs[:2]
        out, done, sems, scratch = refs[7], refs[8], refs[9], refs[10:]
        parity = lax.axis_index("gy") % 2
        attended = []
        for role in range(ROLES):
            near = [
                (halo[role], inside(axis, around)) for halo, (_, axis) in zip(halos, last)
            ]
            near.append((sides[role][...], inside("gy", around) if role else None))
            held = scratch[3 * role : 3 * role + 3]
            attended.append(
                attend_role(role, near, masks, parts, key_weight, value_weight, held)
            )
        copies = []
        for role in range(ROLES):
            rows = update(residual[role], attended[role], refs[2:5], refs[5:7])
            done[role] = keep_live(rows, own[role, slots : slots + 1, :].astype(F32))
            target = out.at[1 - parity if role == 0 else parity]
            copies.append(pltpu.make_async_copy(done.at[role], target, sems.at[role]))
            copies[-1].start()
        for copy in copies:
            copy.wait()

    outs = shape((bins, slots, width), F32)
    scratch = [pltpu.VMEM((bins, slots, width), F32), pltpu.SemaphoreType.DMA((ROLES,))]
    scratch += late_scratch(slots, width, n + 1) * ROLES
    where = pl.BlockSpec(memory_space=pl.ANY)
    return call(body, outs, [VMEM] * len(args), scratch, out_specs=where)(*args)


def run_one(
    leaving, spans, residual, own, last, sides, around, masks, parts, weights, gains, places
):
    _, slots, width = residual.shape
    tall = slots + HEAD_ROWS
    n = len(last)
    halos = [block for block, _ in last]
    args = [residual, own, *halos, *sides, masks, *parts[0], *parts[1], *weights[1:], *gains]
    args = [places.reshape(1, -1), *args]

    def body(places, residual, own, *refs):
        halos, refs = refs[:n], refs[n:]
        first, second, masks, *refs = refs
        parts, refs = (refs[:4], refs[4:8]), refs[8:]
        key_weight, value_weight = refs[:2]
        outs, scratch = refs[7:-3], refs[-3:]
        parity = lax.axis_index("gy") % 2
        stays = scalar(entry(places[...], 1 - parity)) % spans[1] == lax.axis_index("gz")
        role = jnp.where(stays, 1, 0) if leaving else jnp.where(stays, 0, 1)
        place = scalar(entry(places[...], jnp.where(role == 0, 1 - parity, parity)))
        new_role = jnp.where((place // spans[1]) % 2 == parity, 1, 0)
        ahead = role == 0
        block = jnp.where(ahead, first[...].astype(F32), second[...].astype(F32)).astype(BF16)
        flag = inside("gy", around)
        flag = flag if flag is None else ahead | flag
        near = [(halo[role], inside(axis, around)) for halo, (_, axis) in zip(halos, last)]
        near.append((block, flag))
        attended = attend_role(role, near, masks, parts, key_weight, value_weight, scratch)
        result = update(residual[role], attended, refs[2:5], refs[5:7])
        top = own[role, slots:].astype(F32)
        result = keep_live(result, top[:1])
        line = lax.broadcasted_iota(jnp.int32, (HEAD_ROWS, width), 0)
        outs[0][:slots] = result.astype(BF16)
        outs[0][slots:] = jnp.where(line == 1, new_role.astype(F32), top).astype(BF16)
        if not leaving:
            outs[1][...] = result

    outs = [shape((tall, width), BF16)]
    if not leaving:
        outs.append(shape((slots, width), F32))
    return call(body, outs, [VMEM] * len(args), late_scratch(slots, width, n + 1))(*args)


def choose(role, yes, no):
    return jnp.where(role < 0.5, yes.astype(F32), no.astype(F32))


def settle_body(stay, stayed, came, both, first, second, residual):
    slots = stayed.shape[0]
    stay, came = stay[...], came[...]
    role = stay[slots + 1 : slots + 2].astype(F32)
    for index, single in ((0, first), (1, second)):
        block = choose(role, *((stay, came) if index == 0 else (came, stay))).astype(BF16)
        both[index] = block
        single[...] = block
        rows = stayed[...], came[:slots]
        residual[index] = choose(role, *(rows if index == 0 else rows[::-1]))


def settle(stay, stayed, came):
    slots, width = stayed.shape
    tall = slots + HEAD_ROWS
    outs = [
        shape((ROLES, tall, width), BF16),
        shape((tall, width), BF16),
        shape((tall, width), BF16),
        shape((ROLES, slots, width), F32),
    ]
    return call(settle_body, outs, [VMEM] * 3)(stay, stayed, came)


def relocate(state, counts, dest_bin, bins_y):
    total, slots, width = state.shape
    depth = lax.axis_size("gz")
    targets = dest_bin.reshape(-1)
    peer = targets % depth
    local = targets // depth % bins_y
    order = jnp.arange(total, dtype=jnp.int32)
    earlier = (peer[None, :] == peer[:, None]) & (order[None, :] < order[:, None])
    slot = jnp.sum(earlier.astype(jnp.int32), axis=1)
    capacity = (total + depth - 1) // depth
    outgoing = jnp.zeros((depth, capacity, slots, width), F32).at[peer, slot].set(state)
    outgoing_counts = jnp.zeros((depth, capacity), jnp.int32).at[peer, slot].set(counts)
    outgoing_places = jnp.full((depth, capacity), total, jnp.int32).at[peer, slot].set(local)
    arrived = lax.all_to_all(outgoing.astype(BF16), "gz", 0, 0, tiled=True).astype(F32)
    arrived_counts = lax.all_to_all(outgoing_counts, "gz", 0, 0, tiled=True)
    places = lax.all_to_all(outgoing_places, "gz", 0, 0, tiled=True).reshape(-1)
    moved = jnp.zeros((total, slots, width), F32)
    moved = moved.at[places].set(arrived.reshape(-1, slots, width), mode="drop")
    moved_counts = jnp.zeros((total,), jnp.int32)
    moved_counts = moved_counts.at[places].set(arrived_counts.reshape(-1), mode="drop")
    return moved, moved_counts


def exchange(own, first, second, order, ends, last):
    far, sides = {}, {}
    for axis, parity in order:
        if not swaps(lax.axis_size(axis), parity):
            continue
        how = {"gx": ends[0], "gy": ends[1]}.get(axis)
        block = (first, second)[parity] if axis == "gy" else own
        block = swap(block, axis, parity, how)
        if axis == "gy":
            sides[parity] = block
        else:
            far[axis, parity] = (block, axis if how and parity == 1 else None)
    middle = [far[k] for k in sorted(far) if k not in last]
    return middle, [far[k] for k in sorted(far) if k in last], [sides[0], sides[1]]


def shards(features, occupancy, dest_bin, *rest):
    weights, gains = rest[:6], [g.reshape(1, -1) for g in rest[6:]]
    slots, width = features.shape[3:]
    state = features.reshape(2, slots, width)
    counts = occupancy.reshape(2)
    places = dest_bin.reshape(2)
    depth = lax.axis_size("gz")
    spans = (2 * lax.axis_size("gy"), depth)

    def finish(own, residual, beside, far, last, sides, ends):
        around = bool(ends[1])
        masks, first = run_early(own, beside, weights)
        second = run_middle(far, masks, weights, True)
        return residual, own, last, sides, around, masks, (first, second), weights, gains

    ready = prepare(slots, width)
    own, first, second, residual = pack(state, counts, ready)
    far = exchange(own, first, second, ORDERS[0], ENDS[0], LAST[0])
    known = finish(own, residual, [], *far, ENDS[0])
    if depth == 2:
        (leave,) = run_one(True, spans, *known, places)
        came = swap(leave, "gz", 0, None)
        stay, stayed = run_one(False, spans, *known, places)
        peer = swap(stay, "gz", 0, None)
        own, first, second, residual = settle(stay, stayed, came)
        beside = [peer, leave]
        order = [k for k in ORDERS[1] if k[0] != "gz"]
    else:
        state = run_bins(*known)
    if depth != 2:
        state, counts = relocate(state, counts, places, 2)
        own, first, second, residual = pack(state, counts, ready)
        beside, order = [], ORDERS[1]
    far = exchange(own, first, second, order, ENDS[1], LAST[1])
    out = run_bins(*finish(own, residual, beside, *far, ENDS[1]))
    return out.reshape(features.shape)


def solution(mesh):
    placed = (
        P("gx", "gy", "gz", None, None),
        P("gx", "gy", "gz"),
        P("gx", "gy", "gz"),
        *([P()] * 8),
    )
    return jax.shard_map(
        shards,
        mesh=mesh,
        in_specs=placed,
        out_specs=P("gx", "gy", "gz", None, None),
        check_vma=False,
    )
```
